128 devices in a mesh: row: 16 (over z, x), col: 8 (over y, core).
Axes of the slice: x: 4, y: 4, z: 4, core: 2. Of those that a mesh axis runs over, the one named last changes fastest.
Arguments:
- tokens: bfloat16 [2048, 4096], P('row', 'col'), may hold values from -6 to 6
- up_weight: bfloat16 [128, 8, 128, 128], P(('col', 'row')), may hold values from -0.1875 to 0.1875
- up_rows: int32 [128, 8], P('col'), may hold values from 0 to 31, as said below
- down_weight: bfloat16 [128, 8, 128, 128], P(('col', 'row')), may hold values from -0.09375 to 0.09375
- down_cols: int32 [128, 8], P('col'), may hold values from 0 to 31, as said below
- grad_out: bfloat16 [2048, 4096], P('row', 'col'), may hold values from -6 to 6
Outputs:
- layer_out: bfloat16 [2048, 4096], P('row', 'col')
- grad_tokens: bfloat16 [2048, 4096], P('row', 'col')
- grad_up: bfloat16 [128, 8, 128, 128], P(('col', 'row'))
- grad_down: bfloat16 [128, 8, 128, 128], P(('col', 'row'))
The draws below stay inside these ranges and needn't reach their ends.
Inputs may be any that keep to these rules, and one draw needn't show every extreme that they name: `up_rows`: row j lists 8 distinct block rows of the up projection's block column j in rising order; they are that block column's only nonzero blocks. `down_cols`: row i lists 8 distinct block columns of the down projection's block row i in rising order; they are that block row's only nonzero blocks.
All inputs are finite; a program needn't handle non-finite values.
Results may differ from the reference program's by a relative error of at most 0.019.
Values may be sent and summed in bfloat16 or wider, within the bound.
No kernel may reach another device: no remote copies, remote signals or barrier semaphores. Data moves between devices by JAX's collectives and lax.ppermute only.
A program may use at most 128 MiB of HBM per device.

```python
import math
import jax
import jax.numpy as jnp
from jax import lax

D = 4096
FF = 16384
BLK = 128
TOK_ROWS = 128
FB = 128
SLOTS = 8
TOKENS = 2048
N_ROW = 16
N_COL = 8


def distinct_lists(base_key, list_count, value_limit, pick_count):
    row_keys = jax.random.split(base_key, list_count)

    def one_list(row_key):
        return jnp.sort(jax.random.permutation(row_key, value_limit)[:pick_count])
    return jax.vmap(one_list)(row_keys).astype(jnp.int32)


def draw_up_rows(key, part):
    return distinct_lists(jax.random.fold_in(key, 11), FF // BLK, D // BLK, D // BLK // 4)


def draw_down_cols(key, part):
    return distinct_lists(jax.random.fold_in(key, 23), FF // BLK, D // BLK, D // BLK // 4)


def block_levels(stream_key, dims, shards, low, top_value):
    def one(axis_at, blocks):
        steps = jax.random.uniform(jax.random.fold_in(jax.random.fold_in(stream_key, 6), axis_at), (blocks,), jnp.float32, low / len(shards), top_value / len(shards))
        return jnp.repeat(jnp.exp(steps), dims[axis_at] // blocks).reshape((-1,) + (1,) * (len(dims) - axis_at - 1))

    gain = one(*shards[0])
    for cut in shards[1:]:
        gain = gain * one(*cut)
    return gain


def gaussian(key, shape, spread, limit, shards=(), kind=jnp.bfloat16):
    drawn = spread * jax.random.normal(key, shape, jnp.float32)
    if shards:
        drawn = drawn * block_levels(key, shape, shards, -0.22, 0.18)
    return jnp.clip(drawn, -limit, limit).astype(kind)


def setup_inputs(seed: int = 0) -> dict:
    arg_keys = jax.random.split(jax.random.key(seed), 7)
    tokens = gaussian(arg_keys[0], (TOKENS, D), 1.0, 6.0, ((0, 16), (1, 8)))
    up_weight = gaussian(arg_keys[1], (FB, SLOTS, BLK, BLK), (SLOTS * BLK) ** -0.5, 0.1875, ((0, 128),))
    up_rows = draw_up_rows(jax.random.fold_in(arg_keys[6], 71), 0)
    down_weight = gaussian(arg_keys[3], (FB, SLOTS, BLK, BLK), (FF // 4) ** -0.5, 0.09375, ((0, 128),))
    down_cols = draw_down_cols(jax.random.fold_in(arg_keys[6], 71), 0)
    grad_out = gaussian(arg_keys[5], (TOKENS, D), 1.0, 6.0, ((0, 16), (1, 8)))
    return dict(tokens=tokens, up_weight=up_weight, up_rows=up_rows, down_weight=down_weight, down_cols=down_cols, grad_out=grad_out)


def gelu_tanh(values):
    return jax.nn.gelu(values, approximate=True)

def rounded(values):
    return lax.optimization_barrier(values.astype(jnp.bfloat16)).astype(jnp.float32)

def reference(tokens, up_weight, up_rows, down_weight, down_cols, grad_out):
    precise = lax.Precision.HIGHEST
    block_count = D // BLK
    column_blocks = FF // BLK
    panel_width = column_blocks // N_COL
    up_full = up_weight.astype(jnp.float32)
    down_full = down_weight.astype(jnp.float32)
    panel_index = jnp.broadcast_to(jnp.arange(N_COL, dtype=jnp.int32)[:, None], (N_COL, panel_width))
    up_panels = up_rows.reshape(N_COL, panel_width, SLOTS)
    down_panels = down_cols.reshape(N_COL, panel_width, SLOTS)

    def one_group(carried, group_data):
        up_total, down_total = carried
        group_tokens, group_grads = group_data
        token_blocks = group_tokens.astype(jnp.float32).reshape(TOK_ROWS, block_count, BLK)
        grad_blocks = group_grads.astype(jnp.float32).reshape(TOK_ROWS, block_count, BLK)
        pre_act = jnp.zeros((TOK_ROWS, column_blocks, BLK), jnp.float32)
        for slot_index in range(SLOTS):
            picked = token_blocks[:, up_rows[:, slot_index]]
            pre_act = pre_act + jnp.einsum('tja,jab->tjb', picked, up_full[:, slot_index], precision=precise)
        hidden = gelu_tanh(pre_act).astype(jnp.bfloat16)
        hidden_full = hidden.astype(jnp.float32)
        hidden_panels = hidden_full.reshape(TOK_ROWS, N_COL, panel_width, BLK)
        out_parts = jnp.zeros((TOK_ROWS, N_COL, block_count, BLK), jnp.float32)
        grad_hidden = jnp.zeros((TOK_ROWS, column_blocks, BLK), jnp.float32)
        for slot_index in range(SLOTS):
            weight_slot = down_full[:, slot_index]
            product = jnp.einsum('tcia,ciab->tcib', hidden_panels, weight_slot.reshape(N_COL, panel_width, BLK, BLK), precision=precise)
            out_parts = out_parts.at[:, panel_index, down_panels[:, :, slot_index], :].add(product)
            picked = grad_blocks[:, down_cols[:, slot_index]]
            grad_hidden = grad_hidden + jnp.einsum('tib,iab->tia', picked, weight_slot, precision=precise)
        layer_out = lax.optimization_barrier(jnp.sum(rounded(out_parts), axis=1)).astype(jnp.bfloat16).reshape(TOK_ROWS, D)
        pull_back = jax.vjp(gelu_tanh, pre_act)[1]
        grad_pre = pull_back(grad_hidden)[0].astype(jnp.bfloat16)
        grad_full = grad_pre.astype(jnp.float32)
        grad_panels = grad_full.reshape(TOK_ROWS, N_COL, panel_width, BLK)
        input_parts = jnp.zeros((TOK_ROWS, N_COL, block_count, BLK), jnp.float32)
        up_terms = []
        down_terms = []
        for slot_index in range(SLOTS):
            product = jnp.einsum('tcjb,cjab->tcja', grad_panels, up_full[:, slot_index].reshape(N_COL, panel_width, BLK, BLK), precision=precise)
            input_parts = input_parts.at[:, panel_index, up_panels[:, :, slot_index], :].add(product)
            picked = token_blocks[:, up_rows[:, slot_index]]
            up_terms.append(jnp.einsum('tja,tjb->jab', picked, grad_full, precision=precise))
            picked_grad = grad_blocks[:, down_cols[:, slot_index]]
            down_terms.append(jnp.einsum('tia,tib->iab', hidden_full, picked_grad, precision=precise))
        grad_tokens = lax.optimization_barrier(jnp.sum(rounded(input_parts), axis=1)).astype(jnp.bfloat16).reshape(TOK_ROWS, D)
        up_total = up_total + rounded(jnp.stack(up_terms, axis=1))
        down_total = down_total + rounded(jnp.stack(down_terms, axis=1))
        return ((up_total, down_total), (layer_out, grad_tokens))
    start_totals = (jnp.zeros((column_blocks, SLOTS, BLK, BLK), jnp.float32), jnp.zeros((column_blocks, SLOTS, BLK, BLK), jnp.float32))
    grouped = (tokens.reshape(N_ROW, TOK_ROWS, D), grad_out.reshape(N_ROW, TOK_ROWS, D))
    totals, stacked = lax.scan(one_group, start_totals, grouped)
    factor = 1.0 / math.sqrt(TOKENS)
    layer_out = stacked[0].reshape(TOKENS, D)
    grad_tokens = stacked[1].reshape(TOKENS, D)
    grad_up = (totals[0] * factor).astype(jnp.bfloat16)
    grad_down = (totals[1] * factor).astype(jnp.bfloat16)
    return (layer_out, grad_tokens, grad_up, grad_down)
```

```python
import functools
import math

import jax
import jax.numpy as jnp
from jax import lax
from jax.experimental import pallas as pl
from jax.experimental.pallas import tpu as pltpu
from jax.sharding import Mesh
from jax.sharding import PartitionSpec as P

RING = 4
BLK = 128
SHIFTS = (1, 3, 2)
GELU_SCALE = math.sqrt(2.0 / math.pi)
GELU_CUBIC = 0.044715


def shift(values, axis, step):
    return lax.ppermute(values, axis, [(i, (i + step) % RING) for i in range(RING)])


def swap(values):
    return lax.ppermute(values, "core", [(0, 1), (1, 0)])


def ring_gather(values, axis):
    slots = {0: values}
    for step in SHIFTS:
        slots[step] = shift(values, axis, step)
    return [slots[step] for step in range(RING)]


def ring_reduce(chunks, axis):
    parts = [chunks[0]]
    for step in SHIFTS:
        parts.append(shift(chunks[step], axis, RING - step))
    return sum(part.astype(jnp.float32) for part in parts)


def layer_kernel(
    core_ref,
    codes_ref,
    t0, t1, t2, t3,
    g0, g1, g2, g3,
    w_hbm,
    o0, o1, o2, o3,
    i0, i1, i2, i3,
    wg_hbm,
    tok, grd, wgt, out_acc, in_acc, out_st, in_st, wg_st, sems,
):
    core = core_ref[0]
    copies = []
    for ys, src in enumerate((t0, t1, t2, t3)):
        for r in range(2):
            copies.append((src.at[:, r], tok.at[ys * 2 + r]))
    for xs, src in enumerate((g0, g1, g2, g3)):
        copies.append((src, grd.at[:, xs]))
    copies.append((w_hbm, wgt))
    copies = [
        pltpu.make_async_copy(src, dst, sems.at[n]) for n, (src, dst) in enumerate(copies)
    ]
    for copy in copies:
        copy.start()
    out_acc[...] = jnp.zeros_like(out_acc)
    in_acc[...] = jnp.zeros_like(in_acc)
    for copy in copies:
        copy.wait()

    def spot(r, which, z, s):
        code = codes_ref[r, which, z, s]
        return code >> 2, pl.ds(pl.multiple_of((code & 3) * BLK, BLK), BLK)

    def body(step, carry):
        z, r = step >> 1, step & 1
        m = z * 2 + (r ^ core)
        up_spots = [spot(r, 0, z, s) for s in range(8)]
        down_spots = [spot(r, 1, z, s) for s in range(8)]
        picked = jnp.concatenate(
            [tok[a, :, :, c].reshape(256, BLK) for a, c in up_spots], axis=1
        )
        w_up = wgt[m, 0].reshape(8 * BLK, BLK)
        pre = jnp.dot(picked, w_up, preferred_element_type=jnp.float32)
        inner = GELU_SCALE * (pre + GELU_CUBIC * pre * pre * pre)
        t = jnp.tanh(inner)
        hidden = (0.5 * pre * (1.0 + t)).astype(jnp.bfloat16)
        slope = 0.5 * (1.0 + t) + 0.5 * pre * (1.0 - t * t) * GELU_SCALE * (
            1.0 + 3.0 * GELU_CUBIC * pre * pre
        )
        gpicked = jnp.concatenate(
            [grd[a >> 1, :, a & 1, :, c].reshape(256, BLK) for a, c in down_spots], axis=1
        )
        w_down = jnp.concatenate([wgt[m, 1, s] for s in range(8)], axis=1)
        gh = lax.dot_general(
            gpicked, w_down, (((1,), (1,)), ((), ())), preferred_element_type=jnp.float32
        )
        grad_pre = (gh * slope).astype(jnp.bfloat16)
        out_part = jnp.dot(hidden, w_down, preferred_element_type=jnp.float32)
        for s, (a, c) in enumerate(down_spots):
            out_acc[a, :, c] += out_part[:, s * BLK : (s + 1) * BLK]
        dg = lax.dot_general(
            hidden, gpicked, (((0,), (0,)), ((), ())), preferred_element_type=jnp.float32
        ).astype(jnp.bfloat16)
        for s in range(8):
            wg_st[m, 1, s] = dg[:, s * BLK : (s + 1) * BLK]
        in_part = lax.dot_general(
            grad_pre, w_up, (((1,), (1,)), ((), ())), preferred_element_type=jnp.float32
        )
        for s, (a, c) in enumerate(up_spots):
            in_acc[a, :, c] += in_part[:, s * BLK : (s + 1) * BLK]
        ug = lax.dot_general(
            picked, grad_pre, (((0,), (0,)), ((), ())), preferred_element_type=jnp.float32
        ).astype(jnp.bfloat16)
        wg_st[m, 0] = ug.reshape(8, BLK, BLK)
        return carry

    lax.fori_loop(0, 8, body, 0)

    backs = [pltpu.make_async_copy(wg_st, wg_hbm, sems.at[0])]
    backs[0].start()
    for a in range(8):
        out_st[a >> 1, :, a & 1] = out_acc[a].astype(jnp.bfloat16).reshape(4, 64, 512)
    for ys, dst in enumerate((o0, o1, o2, o3)):
        backs.append(pltpu.make_async_copy(out_st.at[ys], dst, sems.at[1 + ys]))
        backs[-1].start()
    for a in range(8):
        in_st[:, a >> 1, a & 1] = in_acc[a].astype(jnp.bfloat16).reshape(4, 64, 512)
    for xs, dst in enumerate((i0, i1, i2, i3)):
        backs.append(pltpu.make_async_copy(in_st.at[xs], dst, sems.at[5 + xs]))
        backs[-1].start()
    for copy in backs:
        copy.wait()


def layer(core, codes, t_slots, g_slots, weights):
    chunk = jax.ShapeDtypeStruct((4, 2, 64, 512), jnp.bfloat16)
    smem = pl.BlockSpec(memory_space=pltpu.SMEM)
    anywhere = pl.BlockSpec(memory_space=pl.ANY)
    results = pl.pallas_call(
        layer_kernel,
        out_shape=[chunk] * 8 + [jax.ShapeDtypeStruct((8, 2, 8, BLK, BLK), jnp.bfloat16)],
        in_specs=[smem, smem] + [anywhere] * 9,
        out_specs=[anywhere] * 9,
        scratch_shapes=[
            pltpu.VMEM((8, 4, 64, 512), jnp.bfloat16),
            pltpu.VMEM((4, 4, 2, 64, 512), jnp.bfloat16),
            pltpu.VMEM((8, 2, 8, BLK, BLK), jnp.bfloat16),
            pltpu.VMEM((8, 256, 512), jnp.float32),
            pltpu.VMEM((8, 256, 512), jnp.float32),
            pltpu.VMEM((4, 4, 2, 64, 512), jnp.bfloat16),
            pltpu.VMEM((4, 4, 2, 64, 512), jnp.bfloat16),
            pltpu.VMEM((8, 2, 8, BLK, BLK), jnp.bfloat16),
            pltpu.SemaphoreType.DMA((13,)),
        ],
        compiler_params=pltpu.CompilerParams(vmem_limit_bytes=48 << 20),
        cost_estimate=pl.CostEstimate(
            flops=3 * 1024**3, bytes_accessed=16 << 20, transcendentals=1 << 18
        ),
        name="layer",
    )(core, codes, *t_slots, *g_slots, weights)
    return results[:4], results[4:8], results[8]


def per_device(tokens, up_weight, up_rows, down_weight, down_cols, grad_out):
    x_at, y_at = lax.axis_index("x"), lax.axis_index("y")
    core = lax.axis_index("core")

    weights = lax.all_gather(
        jnp.stack([up_weight[0], down_weight[0]])[None], ("z", "core"), axis=0, tiled=True
    )

    both = jnp.stack([tokens, grad_out]).reshape(2, 2, 64, 512)
    kept = lax.dynamic_index_in_dim(both, core, axis=1, keepdims=False)
    sent = lax.dynamic_index_in_dim(both, 1 - core, axis=1, keepdims=False)
    came = swap(sent)
    t_own = jnp.stack([kept[0], came[0]])
    g_own = jnp.stack([kept[1], came[1]])

    ids = jnp.stack([up_rows, down_cols]).reshape(2, 4, 4, 8)
    ids = lax.dynamic_index_in_dim(ids, x_at, axis=2, keepdims=False)
    ids = jnp.stack([ids, swap(ids)])
    place = ((y_at - (ids >> 3)) & 3) * 2 + (((ids >> 2) & 1) ^ core)
    codes = place * 4 + (ids & 3)

    t_x = jnp.stack(ring_gather(t_own, "x"))
    g_y = jnp.stack(ring_gather(g_own, "y"))
    t_slots = ring_gather(t_x, "y")
    g_slots = ring_gather(g_y, "x")

    out_chunks, in_chunks, weight_grads = layer(
        core.reshape(1), codes, t_slots, g_slots, weights
    )

    summed = lax.psum_scatter(weight_grads, ("z", "core"), scatter_dimension=0, tiled=True)
    grad_scale = 1.0 / math.sqrt(tokens.shape[0] * lax.axis_size("z") * lax.axis_size("x"))
    scaled = (summed.astype(jnp.float32) * grad_scale).astype(jnp.bfloat16)

    out_y = ring_reduce(out_chunks, "y").astype(jnp.bfloat16)
    in_x = ring_reduce(in_chunks, "x").astype(jnp.bfloat16)
    out_all = ring_reduce([out_y[n] for n in range(RING)], "x").astype(jnp.bfloat16)
    in_all = ring_reduce([in_x[n] for n in range(RING)], "y").astype(jnp.bfloat16)
    mine = jnp.stack([out_all[0], in_all[0]])
    theirs = swap(jnp.stack([out_all[1], in_all[1]]))
    first = jnp.where(core == 0, mine, theirs)
    second = jnp.where(core == 0, theirs, mine)
    acts = jnp.concatenate([first, second], axis=1)
    return (acts[0], acts[1], scaled[:, 0], scaled[:, 1])


def solution(mesh):
    grid = Mesh(mesh.devices.reshape(4, 4, 4, 2), ("z", "x", "y", "core"))
    row, col = ("z", "x"), ("y", "core")
    acts, ids = P(row, col), P(col, None)
    blocks = P(col + row, None, None, None)
    return jax.shard_map(
        per_device,
        mesh=grid,
        in_specs=(acts, blocks, ids, blocks, ids, acts),
        out_specs=(acts, acts, blocks, blocks),
        check_vma=False,
    )
```

```python
import math

import jax
import jax.numpy as jnp
from jax import lax
from jax.experimental import pallas as pl
from jax.experimental.pallas import tpu as pltpu
from jax.sharding import Mesh
from jax.sharding import PartitionSpec as P

RING = 4
BLK = 128
STEPS = (1, 3, 2)
GELU_SCALE = math.sqrt(2.0 / math.pi)
GELU_CUBIC = 0.044715
MIXED = ("x", "y", "core")


def place(x, y, core):
    return (x % RING * RING + y % RING) * 2 + core


def mixed_pairs(step, first):
    pairs = []
    for x in range(RING):
        for y in range(RING):
            for core in range(2):
                dx, dy = (step, 0) if (core == 0) == first else (0, step)
                pairs.append((place(x, y, core), place(x + dx, y + dy, core)))
    return pairs


def mixed_shift(values, step, first):
    return lax.ppermute(values, MIXED, mixed_pairs(step, first))


def z_shift(values, step):
    return lax.ppermute(values, "z", [(i, (i + step) % RING) for i in range(RING)])


def swap(values):
    return lax.ppermute(values, "core", [(0, 1), (1, 0)])


def gather(values, shift):
    slots = {0: values}
    for step in STEPS:
        slots[step] = shift(values, step)
    return [slots[step] for step in range(RING)]


def reduce(chunks, shift):
    parts = [chunks[0]]
    for step in STEPS:
        parts.append(shift(chunks[step], RING - step))
    return sum(part.astype(jnp.float32) for part in parts)


def load(acts_refs, weight_refs, acts, weights, sems):
    copies = [(src, acts.at[n]) for n, src in enumerate(acts_refs)]
    copies += [(src, weights.at[n]) for n, src in enumerate(weight_refs)]
    copies = [
        pltpu.make_async_copy(src, dst, sems.at[n]) for n, (src, dst) in enumerate(copies)
    ]
    for copy in copies:
        copy.start()
    return copies


def spots(where_ref, codes_ref, d, r):
    core, z = where_ref[0], where_ref[1]
    out = []
    for s in range(8):
        code = codes_ref[r, (z - d) & 3, s]
        slot = code >> 3
        first = jnp.where(core == 0, slot * 4, slot)
        cols = pl.ds(pl.multiple_of((code & 3) * BLK, BLK), BLK)
        out.append((first, (code >> 2) & 1, cols))
    return out, jnp.where(core == 0, 1, 4)


def pick(acts, picked, places, stride):
    for s, (first, half, cols) in enumerate(places):
        for q in range(RING):
            picked[q * BLK : (q + 1) * BLK, s * BLK : (s + 1) * BLK] = acts[
                (first + q * stride) >> 2, (first + q * stride) & 3, half, :, cols
            ]


def enter_kernel(
    where_ref, codes_ref, a0, a1, a2, a3, w0, w1, w2, w3, out, acts, weights, picked, sems
):
    core = where_ref[0]
    for copy in load((a0, a1, a2, a3), (w0, w1, w2, w3), acts, weights, sems):
        copy.wait()

    def body(step, carry):
        d, r = step >> 1, step & 1
        places, stride = spots(where_ref, codes_ref, d, r)
        pick(acts, picked, places, stride)

        @pl.when(core == 0)
        def _():
            out[step ^ core] = jnp.dot(
                picked[...],
                weights[d, r].reshape(8 * BLK, BLK),
                preferred_element_type=jnp.float32,
            )

        @pl.when(core == 1)
        def _():
            flat = jnp.concatenate([weights[d, r, s] for s in range(8)], axis=1)
            out[step ^ core] = lax.dot_general(
                picked[...], flat, (((1,), (1,)), ((), ())), preferred_element_type=jnp.float32
            )

        return carry

    lax.fori_loop(0, 8, body, 0)


def leave_kernel(
    where_ref, codes_ref, left, a0, a1, a2, a3, w0, w1, w2, w3,
    o0, o1, o2, o3, g0, g1, g2, g3,
    acts, weights, picked, acc, out, grads, sems,
):
    core = where_ref[0]
    copies = load((a0, a1, a2, a3), (w0, w1, w2, w3), acts, weights, sems)
    acc[...] = jnp.zeros_like(acc)
    for copy in copies:
        copy.wait()

    def body(step, carry):
        d, r = step >> 1, step & 1
        places, stride = spots(where_ref, codes_ref, d, r)
        pick(acts, picked, places, stride)
        mine = left[step ^ core]

        def scatter(s, product):
            for n in range(2):
                first, half, cols = places[s + n]
                for q in range(RING):
                    at = first + q * stride
                    acc[at >> 2, at & 3, half, :, cols] += product[
                        q * BLK : (q + 1) * BLK, n * BLK : (n + 1) * BLK
                    ]

        @pl.when(core == 0)
        def _():
            for s in range(0, 8, 2):
                pair = weights[d, r, s : s + 2].reshape(2 * BLK, BLK)
                scatter(
                    s,
                    lax.dot_general(
                        mine, pair, (((1,), (1,)), ((), ())), preferred_element_type=jnp.float32
                    ),
                )
            grad = lax.dot_general(
                picked[...], mine, (((0,), (0,)), ((), ())), preferred_element_type=jnp.float32
            )
            grads[d, r] = grad.astype(jnp.bfloat16).reshape(8, BLK, BLK)

        @pl.when(core == 1)
        def _():
            for s in range(0, 8, 2):
                pair = jnp.concatenate([weights[d, r, s], weights[d, r, s + 1]], axis=1)
                scatter(s, jnp.dot(mine, pair, preferred_element_type=jnp.float32))
            grad = lax.dot_general(
                mine, picked[...], (((0,), (0,)), ((), ())), preferred_element_type=jnp.float32
            ).astype(jnp.bfloat16)
            for s in range(8):
                grads[d, r, s] = grad[:, s * BLK : (s + 1) * BLK]

        return carry

    lax.fori_loop(0, 8, body, 0)
    backs = []
    for n, dst in enumerate((g0, g1, g2, g3)):
        backs.append(pltpu.make_async_copy(grads.at[n], dst, sems.at[n]))
        backs[-1].start()
    for n, dst in enumerate((o0, o1, o2, o3)):
        out[n] = acc[n].astype(jnp.bfloat16)
        backs.append(pltpu.make_async_copy(out.at[n], dst, sems.at[4 + n]))
        backs[-1].start()
    for copy in backs:
        copy.wait()


SMEM = pl.BlockSpec(memory_space=pltpu.SMEM)
VMEM = pl.BlockSpec(memory_space=pltpu.VMEM)
ANY = pl.BlockSpec(memory_space=pl.ANY)
ACTS = (RING, RING, 2, BLK, 512)
WEIGHTS = (RING, 2, 8, BLK, BLK)


def enter(where, codes, acts, weights):
    return pl.pallas_call(
        enter_kernel,
        out_shape=jax.ShapeDtypeStruct((8, 512, BLK), jnp.float32),
        in_specs=[SMEM, SMEM] + [ANY] * 8,
        out_specs=VMEM,
        scratch_shapes=[
            pltpu.VMEM(ACTS, jnp.bfloat16),
            pltpu.VMEM(WEIGHTS, jnp.bfloat16),
            pltpu.VMEM((512, 8 * BLK), jnp.bfloat16),
            pltpu.SemaphoreType.DMA((8,)),
        ],
        compiler_params=pltpu.CompilerParams(vmem_limit_bytes=20 << 20),
        cost_estimate=pl.CostEstimate(
            flops=1 << 30, bytes_accessed=8 << 20, transcendentals=0
        ),
        name="enter",
    )(where, codes, *acts, *weights)


def leave(where, codes, left, acts, weights):
    chunk = jax.ShapeDtypeStruct(ACTS[1:], jnp.bfloat16)
    grad = jax.ShapeDtypeStruct(WEIGHTS[1:], jnp.bfloat16)
    results = pl.pallas_call(
        leave_kernel,
        out_shape=[chunk] * 4 + [grad] * 4,
        in_specs=[SMEM, SMEM, VMEM] + [ANY] * 8,
        out_specs=[ANY] * 8,
        scratch_shapes=[
            pltpu.VMEM(ACTS, jnp.bfloat16),
            pltpu.VMEM(WEIGHTS, jnp.bfloat16),
            pltpu.VMEM((512, 8 * BLK), jnp.bfloat16),
            pltpu.VMEM(ACTS, jnp.float32),
            pltpu.VMEM(ACTS, jnp.bfloat16),
            pltpu.VMEM(WEIGHTS, jnp.bfloat16),
            pltpu.SemaphoreType.DMA((8,)),
        ],
        compiler_params=pltpu.CompilerParams(vmem_limit_bytes=32 << 20),
        cost_estimate=pl.CostEstimate(
            flops=2 << 30, bytes_accessed=12 << 20, transcendentals=0
        ),
        name="leave",
    )(where, codes, left, *acts, *weights)
    return results[:4], results[4:]


def per_device(tokens, up_weight, up_rows, down_weight, down_cols, grad_out):
    x, y, z = (lax.axis_index(name) for name in ("x", "y", "z"))
    core = lax.axis_index("core")
    up = core == 0

    def first(stage):
        return lambda values, step: mixed_shift(values, step, stage)

    kept = jnp.where(up, tokens, grad_out)
    acts = jnp.stack([kept, swap(jnp.where(up, grad_out, tokens))])
    kept = jnp.where(up, up_weight[0], down_weight[0])
    weights = jnp.stack([kept, swap(jnp.where(up, down_weight[0], up_weight[0]))])

    up_ids = lax.dynamic_index_in_dim(up_rows.reshape(4, 4, 8), x, axis=1, keepdims=False)
    down_ids = lax.dynamic_index_in_dim(down_cols.reshape(4, 4, 8), x, axis=1, keepdims=False)
    ids = jnp.stack([jnp.where(up, up_ids, down_ids), swap(jnp.where(up, down_ids, up_ids))])
    codes = ((y - (ids >> 3)) & 3) * 8 + (((ids >> 2) & 1) ^ core) * 4 + (ids & 3)
    where = jnp.stack([core, z])

    acts = gather(jnp.stack(gather(acts, first(True))), first(False))
    weights = gather(weights, z_shift)

    entered = enter(where, codes, acts, weights)
    pre = lax.ppermute(entered, "core", [(0, 1)])
    t = jnp.tanh(GELU_SCALE * (pre + GELU_CUBIC * pre * pre * pre))
    hidden = (0.5 * pre * (1.0 + t)).astype(jnp.bfloat16)
    slope = 0.5 * (1.0 + t) + 0.5 * pre * (1.0 - t * t) * GELU_SCALE * (
        1.0 + 3.0 * GELU_CUBIC * pre * pre
    )
    grad_pre = lax.ppermute((entered * slope).astype(jnp.bfloat16), "core", [(1, 0)])
    chunks, grads = leave(where, codes, jnp.where(up, grad_pre, hidden), acts, weights)

    summed = reduce(chunks, first(False)).astype(jnp.bfloat16)
    final = reduce([summed[n] for n in range(RING)], first(True)).astype(jnp.bfloat16)
    grad_scale = 1.0 / math.sqrt(tokens.shape[0] * lax.axis_size("z") * lax.axis_size("x"))
    scaled = (reduce(grads, z_shift) * grad_scale).astype(jnp.bfloat16)
    came = swap(final[1])
    came_grad = swap(scaled[1])
    layer_out = jnp.where(up, came, final[0])
    grad_tokens = jnp.where(up, final[0], came)
    grad_up = jnp.where(up, scaled[0], came_grad)
    grad_down = jnp.where(up, came_grad, scaled[0])
    return (layer_out, grad_tokens, grad_up[None], grad_down[None])


def solution(mesh):
    grid = Mesh(mesh.devices.reshape(4, 4, 4, 2), ("z", "x", "y", "core"))
    row, col = ("z", "x"), ("y", "core")
    acts, ids = P(row, col), P(col, None)
    blocks = P(col + row, None, None, None)
    return jax.shard_map(
        per_device,
        mesh=grid,
        in_specs=(acts, blocks, ids, blocks, ids, acts),
        out_specs=(acts, acts, blocks, blocks),
        check_vma=False,
    )
```

```python
import math

import jax
import jax.numpy as jnp
from jax import lax
from jax.experimental import pallas as pl
from jax.experimental.pallas import tpu as pltpu
from jax.sharding import Mesh
from jax.sharding import PartitionSpec as P

RING = 4
BLK = 128
STEPS = (1, 3, 2)
GELU_SCALE = math.sqrt(2.0 / math.pi)
GELU_CUBIC = 0.044715
MIXED = ("x", "y", "core")


def place(x, y, core):
    return (x % RING * RING + y % RING) * 2 + core


def mixed_pairs(step, first):
    pairs = []
    for x in range(RING):
        for y in range(RING):
            for core in range(2):
                dx, dy = (step, 0) if (core == 0) == first else (0, step)
                pairs.append((place(x, y, core), place(x + dx, y + dy, core)))
    return pairs


def mixed_shift(values, step, first):
    return lax.ppermute(values, MIXED, mixed_pairs(step, first))


def z_shift(values, step):
    return lax.ppermute(values, "z", [(i, (i + step) % RING) for i in range(RING)])


def swap(values):
    return lax.ppermute(values, "core", [(0, 1), (1, 0)])


def gather(values, shift):
    slots = {0: values}
    for step in STEPS:
        slots[step] = shift(values, step)
    return [slots[step] for step in range(RING)]


def reduce(chunks, shift):
    parts = [chunks[0]]
    for step in STEPS:
        parts.append(shift(chunks[step], RING - step))
    return sum(part.astype(jnp.float32) for part in parts)


def load(acts_refs, weight_refs, acts, weights, sems):
    copies = [(src, acts.at[n]) for n, src in enumerate(acts_refs)]
    copies += [(src, weights.at[n]) for n, src in enumerate(weight_refs)]
    copies = [
        pltpu.make_async_copy(src, dst, sems.at[n]) for n, (src, dst) in enumerate(copies)
    ]
    for copy in copies:
        copy.start()
    return copies


def spots(where_ref, codes_ref, d, r):
    core, z = where_ref[0], where_ref[1]
    out = []
    for s in range(8):
        code = codes_ref[r, (z - d) & 3, s]
        slot = code >> 3
        first = jnp.where(core == 0, slot * 4, slot)
        cols = pl.ds(pl.multiple_of((code & 3) * BLK, BLK), BLK)
        out.append((first, (code >> 2) & 1, cols))
    return out, jnp.where(core == 0, 1, 4)


def pick(acts, picked, places, stride):
    for s, (first, half, cols) in enumerate(places):
        for q in range(RING):
            picked[q * BLK : (q + 1) * BLK, s * BLK : (s + 1) * BLK] = acts[
                (first + q * stride) >> 2, (first + q * stride) & 3, half, :, cols
            ]


def enter_kernel(
    where_ref, codes_ref, a0, a1, a2, a3, w0, w1, w2, w3,
    acts, weights, sent, slope, picked, sems,
):
    core = where_ref[0]
    for copy in load((a0, a1, a2, a3), (w0, w1, w2, w3), acts, weights, sems):
        copy.wait()

    def body(step, carry):
        d, r = step >> 1, step & 1
        places, stride = spots(where_ref, codes_ref, d, r)
        pick(acts, picked, places, stride)

        @pl.when(core == 0)
        def _():
            pre = jnp.dot(
                picked[...],
                weights[d, r].reshape(8 * BLK, BLK),
                preferred_element_type=jnp.float32,
            )
            t = jnp.tanh(GELU_SCALE * (pre + GELU_CUBIC * pre * pre * pre))
            sent[step] = (0.5 * pre * (1.0 + t)).astype(jnp.bfloat16)
            slope[step] = 0.5 * (1.0 + t) + 0.5 * pre * (1.0 - t * t) * GELU_SCALE * (
                1.0 + 3.0 * GELU_CUBIC * pre * pre
            )

        @pl.when(core == 1)
        def _():
            flat = jnp.concatenate([weights[d, r, s] for s in range(8)], axis=1)
            sent[step ^ 1] = lax.dot_general(
                picked[...], flat, (((1,), (1,)), ((), ())), preferred_element_type=jnp.float32
            ).astype(jnp.bfloat16)

        return carry

    lax.fori_loop(0, 8, body, 0)


def pulled(came, slope, step):
    return (came[step].astype(jnp.float32) * slope[step]).astype(jnp.bfloat16)


def sums_kernel(where_ref, codes_ref, weights, came, slope, o0, o1, o2, o3, acc):
    core = where_ref[0]
    acc[...] = jnp.zeros_like(acc)

    def body(step, carry):
        d, r = step >> 1, step & 1
        places, stride = spots(where_ref, codes_ref, d, r)

        def scatter(s, product):
            for n in range(2):
                first, half, cols = places[s + n]
                for q in range(RING):
                    at = first + q * stride
                    acc[at >> 2, at & 3, half, :, cols] += product[
                        q * BLK : (q + 1) * BLK, n * BLK : (n + 1) * BLK
                    ]

        @pl.when(core == 0)
        def _():
            mine = pulled(came, slope, step)
            for s in range(0, 8, 2):
                pair = weights[d, r, s : s + 2].reshape(2 * BLK, BLK)
                scatter(
                    s,
                    lax.dot_general(
                        mine, pair, (((1,), (1,)), ((), ())), preferred_element_type=jnp.float32
                    ),
                )

        @pl.when(core == 1)
        def _():
            mine = came[step ^ 1]
            for s in range(0, 8, 2):
                pair = jnp.concatenate([weights[d, r, s], weights[d, r, s + 1]], axis=1)
                scatter(s, jnp.dot(mine, pair, preferred_element_type=jnp.float32))

        return carry

    lax.fori_loop(0, 8, body, 0)
    for n, out in enumerate((o0, o1, o2, o3)):
        out[...] = acc[n].astype(jnp.bfloat16)


def grads_kernel(where_ref, codes_ref, acts, came, slope, g0, g1, g2, g3, picked):
    core = where_ref[0]
    for d, grads in enumerate((g0, g1, g2, g3)):

        def body(r, carry):
            step = d * 2 + r
            places, stride = spots(where_ref, codes_ref, d, r)
            pick(acts, picked, places, stride)

            @pl.when(core == 0)
            def _():
                grad = lax.dot_general(
                    picked[...],
                    pulled(came, slope, step),
                    (((0,), (0,)), ((), ())),
                    preferred_element_type=jnp.float32,
                )
                grads[r] = grad.astype(jnp.bfloat16).reshape(8, BLK, BLK)

            @pl.when(core == 1)
            def _():
                grad = lax.dot_general(
                    came[step ^ 1],
                    picked[...],
                    (((0,), (0,)), ((), ())),
                    preferred_element_type=jnp.float32,
                ).astype(jnp.bfloat16)
                for s in range(8):
                    grads[r, s] = grad[:, s * BLK : (s + 1) * BLK]

            return carry

        lax.fori_loop(0, 2, body, 0)


SMEM = pl.BlockSpec(memory_space=pltpu.SMEM)
VMEM = pl.BlockSpec(memory_space=pltpu.VMEM)
ANY = pl.BlockSpec(memory_space=pl.ANY)
ACTS = (RING, RING, 2, BLK, 512)
WEIGHTS = (RING, 2, 8, BLK, BLK)


CHUNK = jax.ShapeDtypeStruct(ACTS[1:], jnp.bfloat16)
GRAD = jax.ShapeDtypeStruct(WEIGHTS[1:], jnp.bfloat16)
HIDDEN = (8, 512, BLK)


def cost(flops, moved):
    return pl.CostEstimate(flops=flops, bytes_accessed=moved, transcendentals=0)


def enter(where, codes, acts, weights):
    return pl.pallas_call(
        enter_kernel,
        out_shape=[
            jax.ShapeDtypeStruct(ACTS, jnp.bfloat16),
            jax.ShapeDtypeStruct(WEIGHTS, jnp.bfloat16),
            jax.ShapeDtypeStruct(HIDDEN, jnp.bfloat16),
            jax.ShapeDtypeStruct(HIDDEN, jnp.float32),
        ],
        in_specs=[SMEM, SMEM] + [ANY] * 8,
        out_specs=[VMEM] * 4,
        scratch_shapes=[
            pltpu.VMEM((512, 8 * BLK), jnp.bfloat16),
            pltpu.SemaphoreType.DMA((8,)),
        ],
        compiler_params=pltpu.CompilerParams(vmem_limit_bytes=16 << 20),
        cost_estimate=cost(1 << 30, 8 << 20),
        name="enter",
    )(where, codes, *acts, *weights)


def sums(where, codes, weights, came, slope):
    return pl.pallas_call(
        sums_kernel,
        out_shape=[CHUNK] * 4,
        in_specs=[SMEM, SMEM] + [VMEM] * 3,
        out_specs=[VMEM] * 4,
        scratch_shapes=[pltpu.VMEM(ACTS, jnp.float32)],
        compiler_params=pltpu.CompilerParams(vmem_limit_bytes=24 << 20),
        cost_estimate=cost(1 << 30, 8 << 20),
        name="sums",
    )(where, codes, weights, came, slope)


def block_grads(where, codes, acts, came, slope):
    return pl.pallas_call(
        grads_kernel,
        out_shape=[GRAD] * 4,
        in_specs=[SMEM, SMEM] + [VMEM] * 3,
        out_specs=[VMEM] * 4,
        scratch_shapes=[pltpu.VMEM((512, 8 * BLK), jnp.bfloat16)],
        compiler_params=pltpu.CompilerParams(vmem_limit_bytes=16 << 20),
        cost_estimate=cost(1 << 30, 8 << 20),
        name="grads",
    )(where, codes, acts, came, slope)


def per_device(tokens, up_weight, up_rows, down_weight, down_cols, grad_out):
    x, y, z = (lax.axis_index(name) for name in ("x", "y", "z"))
    core = lax.axis_index("core")
    up = core == 0

    def first(stage):
        return lambda values, step: mixed_shift(values, step, stage)

    kept = jnp.where(up, tokens, grad_out)
    acts = jnp.stack([kept, swap(jnp.where(up, grad_out, tokens))])
    kept = jnp.where(up, up_weight[0], down_weight[0])
    weights = jnp.stack([kept, swap(jnp.where(up, down_weight[0], up_weight[0]))])

    up_ids = lax.dynamic_index_in_dim(up_rows.reshape(4, 4, 8), x, axis=1, keepdims=False)
    down_ids = lax.dynamic_index_in_dim(down_cols.reshape(4, 4, 8), x, axis=1, keepdims=False)
    ids = jnp.stack([jnp.where(up, up_ids, down_ids), swap(jnp.where(up, down_ids, up_ids))])
    codes = ((y - (ids >> 3)) & 3) * 8 + (((ids >> 2) & 1) ^ core) * 4 + (ids & 3)
    where = jnp.stack([core, z])

    acts = gather(jnp.stack(gather(acts, first(True))), first(False))
    weights = gather(weights, z_shift)

    acts, weights, sent, slope = enter(where, codes, acts, weights)
    came = swap(sent)
    chunks = sums(where, codes, weights, came, slope)
    grads = block_grads(where, codes, acts, came, slope)

    summed = reduce(chunks, first(False)).astype(jnp.bfloat16)
    final = reduce([summed[n] for n in range(RING)], first(True)).astype(jnp.bfloat16)
    grad_scale = 1.0 / math.sqrt(tokens.shape[0] * lax.axis_size("z") * lax.axis_size("x"))
    scaled = (reduce(grads, z_shift) * grad_scale).astype(jnp.bfloat16)
    came_act = swap(final[1])
    came_grad = swap(scaled[1])
    layer_out = jnp.where(up, came_act, final[0])
    grad_tokens = jnp.where(up, final[0], came_act)
    grad_up = jnp.where(up, scaled[0], came_grad)
    grad_down = jnp.where(up, came_grad, scaled[0])
    return (layer_out, grad_tokens, grad_up[None], grad_down[None])


def solution(mesh):
    grid = Mesh(mesh.devices.reshape(4, 4, 4, 2), ("z", "x", "y", "core"))
    row, col = ("z", "x"), ("y", "core")
    acts, ids = P(row, col), P(col, None)
    blocks = P(col + row, None, None, None)
    return jax.shard_map(
        per_device,
        mesh=grid,
        in_specs=(acts, blocks, ids, blocks, ids, acts),
        out_specs=(acts, acts, blocks, blocks),
        check_vma=False,
    )
```

```python
import functools
import math

import jax
import jax.numpy as jnp
from jax import lax
from jax.experimental import pallas as pl
from jax.experimental.pallas import tpu as pltpu
from jax.sharding import Mesh
from jax.sharding import PartitionSpec as P

RING = 4
BLK = 128
STEPS = (1, 3, 2)
GELU_SCALE = math.sqrt(2.0 / math.pi)
GELU_CUBIC = 0.044715
MIXED = ("x", "y", "core")


def place(x, y, core):
    return (x % RING * RING + y % RING) * 2 + core


def mixed_pairs(step, first):
    pairs = []
    for x in range(RING):
        for y in range(RING):
            for core in range(2):
                dx, dy = (step, 0) if (core == 0) == first else (0, step)
                pairs.append((place(x, y, core), place(x + dx, y + dy, core)))
    return pairs


def mixed_shift(values, step, first):
    return lax.ppermute(values, MIXED, mixed_pairs(step, first))


def z_shift(values, step):
    pairs = [(i * 2, (i + step) % RING * 2) for i in range(RING)]
    pairs += [(i * 2 + 1, (i - step) % RING * 2 + 1) for i in range(RING)]
    return lax.ppermute(values, ("z", "core"), pairs)


def swap(values):
    return lax.ppermute(values, "core", [(0, 1), (1, 0)])


def gather(values, shift):
    slots = {0: values}
    for step in STEPS:
        slots[step] = shift(values, step)
    return [slots[step] for step in range(RING)]


def reduce(chunks, shift):
    parts = [chunks[0]]
    for step in STEPS:
        parts.append(shift(chunks[step], RING - step))
    return sum(part.astype(jnp.float32) for part in parts)


def load(acts_refs, weight_refs, acts, weights, sems):
    copies = [(src, acts.at[n]) for n, src in enumerate(acts_refs)]
    copies += [(src, weights.at[n]) for n, src in enumerate(weight_refs)]
    copies = [
        pltpu.make_async_copy(src, dst, sems.at[n]) for n, (src, dst) in enumerate(copies)
    ]
    for copy in copies:
        copy.start()
    return copies


def from_z(where_ref, d):
    return (where_ref[1] + jnp.where(where_ref[0] == 0, -d, d)) & 3


def column(where_ref, d, r):
    return from_z(where_ref, d) * 2 + (r ^ where_ref[0])


def spots(where_ref, codes_ref, d, r):
    core = where_ref[0]
    z = from_z(where_ref, d)
    out = []
    for s in range(8):
        code = codes_ref[r, z, s]
        slot = code >> 3
        first = jnp.where(core == 0, slot * 4, slot)
        cols = pl.ds(pl.multiple_of((code & 3) * BLK, BLK), BLK)
        out.append((first, (code >> 2) & 1, cols))
    return out, jnp.where(core == 0, 1, 4)


def pick(acts, picked, places, stride):
    for s, (first, half, cols) in enumerate(places):
        for q in range(RING):
            picked[q * BLK : (q + 1) * BLK, s * BLK : (s + 1) * BLK] = acts[
                (first + q * stride) >> 2, (first + q * stride) & 3, half, :, cols
            ]


def enter_kernel(
    where_ref, codes_ref, a0, a1, a2, a3, w0, w1, w2, w3,
    acts, weights, sent, slope, picked, sems,
):
    core = where_ref[0]
    for copy in load((a0, a1, a2, a3), (w0, w1, w2, w3), acts, weights, sems):
        copy.wait()

    def body(step, carry):
        d, r = step >> 1, step & 1
        at = column(where_ref, d, r)
        places, stride = spots(where_ref, codes_ref, d, r)
        pick(acts, picked, places, stride)

        @pl.when(core == 0)
        def _():
            pre = jnp.dot(
                picked[...],
                weights[d, r].reshape(8 * BLK, BLK),
                preferred_element_type=jnp.float32,
            )
            t = jnp.tanh(GELU_SCALE * (pre + GELU_CUBIC * pre * pre * pre))
            sent[at] = (0.5 * pre * (1.0 + t)).astype(jnp.bfloat16)
            slope[at] = 0.5 * (1.0 + t) + 0.5 * pre * (1.0 - t * t) * GELU_SCALE * (
                1.0 + 3.0 * GELU_CUBIC * pre * pre
            )

        @pl.when(core == 1)
        def _():
            flat = jnp.concatenate([weights[d, r, s] for s in range(8)], axis=1)
            sent[at] = lax.dot_general(
                picked[...], flat, (((1,), (1,)), ((), ())), preferred_element_type=jnp.float32
            ).astype(jnp.bfloat16)

        return carry

    lax.fori_loop(0, 8, body, 0)


def pulled(came, slope, step):
    return (came[step].astype(jnp.float32) * slope[step]).astype(jnp.bfloat16)


def sums_kernel(where_ref, codes_ref, weights, came, slope, o0, o1, o2, o3, acc):
    core = where_ref[0]
    acc[...] = jnp.zeros_like(acc)

    def body(step, carry):
        d, r = step >> 1, step & 1
        row = column(where_ref, d, r)
        places, stride = spots(where_ref, codes_ref, d, r)

        def scatter(s, product):
            for n in range(2):
                first, half, cols = places[s + n]
                for q in range(RING):
                    at = first + q * stride
                    acc[at >> 2, at & 3, half, :, cols] += product[
                        q * BLK : (q + 1) * BLK, n * BLK : (n + 1) * BLK
                    ]

        @pl.when(core == 0)
        def _():
            mine = pulled(came, slope, row)
            for s in range(0, 8, 2):
                pair = weights[d, r, s : s + 2].reshape(2 * BLK, BLK)
                scatter(
                    s,
                    lax.dot_general(
                        mine, pair, (((1,), (1,)), ((), ())), preferred_element_type=jnp.float32
                    ),
                )

        @pl.when(core == 1)
        def _():
            mine = came[row]
            for s in range(0, 8, 2):
                pair = jnp.concatenate([weights[d, r, s], weights[d, r, s + 1]], axis=1)
                scatter(s, jnp.dot(mine, pair, preferred_element_type=jnp.float32))

        return carry

    lax.fori_loop(0, 8, body, 0)
    for n, out in enumerate((o0, o1, o2, o3)):
        out[...] = acc[n].astype(jnp.bfloat16)


def grads_kernel(slots, where_ref, codes_ref, acts, came, slope, *refs):
    core = where_ref[0]
    picked = refs[-1]
    for d, grads in zip(slots, refs):

        def body(r, carry):
            row = column(where_ref, d, r)
            places, stride = spots(where_ref, codes_ref, d, r)
            pick(acts, picked, places, stride)

            @pl.when(core == 0)
            def _():
                grad = lax.dot_general(
                    picked[...],
                    pulled(came, slope, row),
                    (((0,), (0,)), ((), ())),
                    preferred_element_type=jnp.float32,
                )
                grads[r] = grad.astype(jnp.bfloat16).reshape(8, BLK, BLK)

            @pl.when(core == 1)
            def _():
                grad = lax.dot_general(
                    came[row],
                    picked[...],
                    (((0,), (0,)), ((), ())),
                    preferred_element_type=jnp.float32,
                ).astype(jnp.bfloat16)
                for s in range(8):
                    grads[r, s] = grad[:, s * BLK : (s + 1) * BLK]

            return carry

        lax.fori_loop(0, 2, body, 0)


SMEM = pl.BlockSpec(memory_space=pltpu.SMEM)
VMEM = pl.BlockSpec(memory_space=pltpu.VMEM)
ANY = pl.BlockSpec(memory_space=pl.ANY)
ACTS = (RING, RING, 2, BLK, 512)
WEIGHTS = (RING, 2, 8, BLK, BLK)


CHUNK = jax.ShapeDtypeStruct(ACTS[1:], jnp.bfloat16)
GRAD = jax.ShapeDtypeStruct(WEIGHTS[1:], jnp.bfloat16)
HIDDEN = (8, 512, BLK)


def cost(flops, moved):
    return pl.CostEstimate(flops=flops, bytes_accessed=moved, transcendentals=0)


def enter(where, codes, acts, weights):
    return pl.pallas_call(
        enter_kernel,
        out_shape=[
            jax.ShapeDtypeStruct(ACTS, jnp.bfloat16),
            jax.ShapeDtypeStruct(WEIGHTS, jnp.bfloat16),
            jax.ShapeDtypeStruct(HIDDEN, jnp.bfloat16),
            jax.ShapeDtypeStruct(HIDDEN, jnp.float32),
        ],
        in_specs=[SMEM, SMEM] + [ANY] * 8,
        out_specs=[VMEM] * 4,
        scratch_shapes=[
            pltpu.VMEM((512, 8 * BLK), jnp.bfloat16),
            pltpu.SemaphoreType.DMA((8,)),
        ],
        compiler_params=pltpu.CompilerParams(vmem_limit_bytes=16 << 20),
        cost_estimate=cost(1 << 30, 8 << 20),
        name="enter",
    )(where, codes, *acts, *weights)


def sums(where, codes, weights, came, slope):
    return pl.pallas_call(
        sums_kernel,
        out_shape=[CHUNK] * 4,
        in_specs=[SMEM, SMEM] + [VMEM] * 3,
        out_specs=[VMEM] * 4,
        scratch_shapes=[pltpu.VMEM(ACTS, jnp.float32)],
        compiler_params=pltpu.CompilerParams(vmem_limit_bytes=24 << 20),
        cost_estimate=cost(1 << 30, 8 << 20),
        name="sums",
    )(where, codes, weights, came, slope)


def block_grads(slots, where, codes, acts, came, slope):
    return pl.pallas_call(
        functools.partial(grads_kernel, slots),
        out_shape=[GRAD] * len(slots),
        in_specs=[SMEM, SMEM] + [VMEM] * 3,
        out_specs=[VMEM] * len(slots),
        scratch_shapes=[pltpu.VMEM((512, 8 * BLK), jnp.bfloat16)],
        compiler_params=pltpu.CompilerParams(vmem_limit_bytes=16 << 20),
        cost_estimate=cost(1 << 29, 8 << 20),
        name="grads",
    )(where, codes, acts, came, slope)


def per_device(tokens, up_weight, up_rows, down_weight, down_cols, grad_out):
    x, y, z = (lax.axis_index(name) for name in ("x", "y", "z"))
    core = lax.axis_index("core")
    up = core == 0

    def first(stage):
        return lambda values, step: mixed_shift(values, step, stage)

    kept = jnp.where(up, tokens, grad_out)
    acts = jnp.stack([kept, swap(jnp.where(up, grad_out, tokens))])
    kept = jnp.where(up, up_weight[0], down_weight[0])
    weights = jnp.stack([kept, swap(jnp.where(up, down_weight[0], up_weight[0]))])

    up_ids = lax.dynamic_index_in_dim(up_rows.reshape(4, 4, 8), x, axis=1, keepdims=False)
    down_ids = lax.dynamic_index_in_dim(down_cols.reshape(4, 4, 8), x, axis=1, keepdims=False)
    ids = jnp.stack([jnp.where(up, up_ids, down_ids), swap(jnp.where(up, down_ids, up_ids))])
    codes = ((y - (ids >> 3)) & 3) * 8 + (((ids >> 2) & 1) ^ core) * 4 + (ids & 3)
    where = jnp.stack([core, z])

    acts = gather(jnp.stack(gather(acts, first(True))), first(False))
    weights = gather(weights, z_shift)

    acts, weights, sent, slope = enter(where, codes, acts, weights)
    came = swap(sent)
    chunks = sums(where, codes, weights, came, slope)
    grads_1, grads_3 = block_grads((1, 3), where, codes, acts, came, slope)
    grads_2, grads_0 = block_grads((2, 0), where, codes, acts, came, slope)
    grads = [grads_0, grads_1, grads_2, grads_3]

    summed = reduce(chunks, first(False)).astype(jnp.bfloat16)
    final = reduce([summed[n] for n in range(RING)], first(True)).astype(jnp.bfloat16)
    grad_scale = 1.0 / math.sqrt(tokens.shape[0] * lax.axis_size("z") * lax.axis_size("x"))
    scaled = (reduce(grads, z_shift) * grad_scale).astype(jnp.bfloat16)
    came_act = swap(final[1])
    came_grad = swap(scaled[1])
    layer_out = jnp.where(up, came_act, final[0])
    grad_tokens = jnp.where(up, final[0], came_act)
    grad_up = jnp.where(up, scaled[0], came_grad)
    grad_down = jnp.where(up, came_grad, scaled[0])
    return (layer_out, grad_tokens, grad_up[None], grad_down[None])


def solution(mesh):
    grid = Mesh(mesh.devices.reshape(4, 4, 4, 2), ("z", "x", "y", "core"))
    row, col = ("z", "x"), ("y", "core")
    acts, ids = P(row, col), P(col, None)
    blocks = P(col + row, None, None, None)
    return jax.shard_map(
        per_device,
        mesh=grid,
        in_specs=(acts, blocks, ids, blocks, ids, acts),
        out_specs=(acts, acts, blocks, blocks),
        check_vma=False,
    )
```

```python
import functools
import math

import jax
import jax.numpy as jnp
from jax import lax
from jax.experimental import pallas as pl
from jax.experimental.pallas import tpu as pltpu
from jax.sharding import Mesh
from jax.sharding import PartitionSpec as P

RING = 4
BLK = 128
STEPS = (1, 3, 2)
GELU_SCALE = math.sqrt(2.0 / math.pi)
GELU_CUBIC = 0.044715
MIXED = ("x", "y", "core")


def place(x, y, core):
    return (x % RING * RING + y % RING) * 2 + core


def mixed_pairs(step, first):
    pairs = []
    for x in range(RING):
        for y in range(RING):
            for core in range(2):
                dx, dy = (step, 0) if (core == 0) == first else (0, step)
                pairs.append((place(x, y, core), place(x + dx, y + dy, core)))
    return pairs


def mixed_shift(values, step, first):
    return lax.ppermute(values, MIXED, mixed_pairs(step, first))


def z_shift(values, step):
    pairs = [(i * 2, (i + step) % RING * 2) for i in range(RING)]
    pairs += [(i * 2 + 1, (i - step) % RING * 2 + 1) for i in range(RING)]
    return lax.ppermute(values, ("z", "core"), pairs)


def swap(values):
    return lax.ppermute(values, "core", [(0, 1), (1, 0)])


def gather(values, shift):
    slots = {0: values}
    for step in STEPS:
        slots[step] = shift(values, step)
    return [slots[step] for step in range(RING)]


def reduce(chunks, shift):
    parts = [chunks[0]]
    for step in STEPS:
        parts.append(shift(chunks[step], RING - step))
    return sum(part.astype(jnp.float32) for part in parts)


def load(acts_refs, weight_refs, acts, weights, sems):
    copies = [(src, acts.at[n]) for n, src in enumerate(acts_refs)]
    copies += [(src, weights.at[n]) for n, src in enumerate(weight_refs)]
    copies = [
        pltpu.make_async_copy(src, dst, sems.at[n]) for n, (src, dst) in enumerate(copies)
    ]
    for copy in copies:
        copy.start()
    return copies


def from_z(where_ref, d):
    return (where_ref[1] + jnp.where(where_ref[0] == 0, -d, d)) & 3


def column(where_ref, d, r):
    return from_z(where_ref, d) * 2 + (r ^ where_ref[0])


def spots(where_ref, codes_ref, d, r):
    core = where_ref[0]
    z = from_z(where_ref, d)
    out = []
    for s in range(8):
        code = codes_ref[r, z, s]
        slot = code >> 3
        first = jnp.where(core == 0, slot * 4, slot)
        cols = pl.ds(pl.multiple_of((code & 3) * BLK, BLK), BLK)
        out.append((first, (code >> 2) & 1, cols))
    return out, jnp.where(core == 0, 1, 4)


def pick(acts, picked, places, stride):
    for s, (first, half, cols) in enumerate(places):
        for q in range(RING):
            picked[q * BLK : (q + 1) * BLK, s * BLK : (s + 1) * BLK] = acts[
                (first + q * stride) >> 2, (first + q * stride) & 3, half, :, cols
            ]


def per_core(where_ref, codes_ref, columns, unroll, for_up, for_down):
    def run(step_function):
        def body(turn, carry):
            for n in range(unroll):
                step = turn * unroll + n
                step_function(columns[0] + (step >> 1), step & 1, n)
            return carry

        lax.fori_loop(0, 2 * len(columns) // unroll, body, 0)

    @pl.when(where_ref[0] == 0)
    def _():
        run(for_up)

    @pl.when(where_ref[0] == 1)
    def _():
        run(for_down)


def enter_kernel(
    where_ref, codes_ref, a0, a1, a2, a3, w0, w1, w2, w3,
    acts, weights, sent, slope, picked, sems,
):
    for copy in load((a0, a1, a2, a3), (w0, w1, w2, w3), acts, weights, sems):
        copy.wait()

    def for_up(d, r, n):
        at = column(where_ref, d, r)
        pick(acts, picked.at[n], *spots(where_ref, codes_ref, d, r))
        pre = jnp.dot(
            picked[n], weights[d, r].reshape(8 * BLK, BLK), preferred_element_type=jnp.float32
        )
        square = pre * pre
        t = jnp.tanh(pre * (GELU_SCALE + GELU_SCALE * GELU_CUBIC * square))
        half = 0.5 + 0.5 * t
        sent[at] = (pre * half).astype(jnp.bfloat16)
        slope[at] = half + pre * (half - half * t) * (
            GELU_SCALE + 3.0 * GELU_SCALE * GELU_CUBIC * square
        )

    def for_down(d, r, n):
        at = column(where_ref, d, r)
        pick(acts, picked.at[n], *spots(where_ref, codes_ref, d, r))
        flat = jnp.concatenate([weights[d, r, s] for s in range(8)], axis=1)
        sent[at] = lax.dot_general(
            picked[n], flat, (((1,), (1,)), ((), ())), preferred_element_type=jnp.float32
        ).astype(jnp.bfloat16)

    per_core(where_ref, codes_ref, range(4), 4, for_up, for_down)


def pulled(came, slope, row):
    return (came[row].astype(jnp.float32) * slope[row]).astype(jnp.bfloat16)


def sums_kernel(where_ref, codes_ref, weights, came, slope, o0, o1, o2, o3, acc):
    acc[...] = jnp.zeros_like(acc)

    def scatter(places, stride, s, product):
        for n in range(2):
            first, half, cols = places[s + n]
            for q in range(RING):
                at = first + q * stride
                acc[at >> 2, at & 3, half, :, cols] += product[
                    q * BLK : (q + 1) * BLK, n * BLK : (n + 1) * BLK
                ]

    def for_up(d, r, n):
        mine = pulled(came, slope, column(where_ref, d, r))
        places, stride = spots(where_ref, codes_ref, d, r)
        for s in range(0, 8, 2):
            pair = weights[d, r, s : s + 2].reshape(2 * BLK, BLK)
            product = lax.dot_general(
                mine, pair, (((1,), (1,)), ((), ())), preferred_element_type=jnp.float32
            )
            scatter(places, stride, s, product)

    def for_down(d, r, n):
        mine = came[column(where_ref, d, r)]
        places, stride = spots(where_ref, codes_ref, d, r)
        for s in range(0, 8, 2):
            pair = jnp.concatenate([weights[d, r, s], weights[d, r, s + 1]], axis=1)
            product = jnp.dot(mine, pair, preferred_element_type=jnp.float32)
            scatter(places, stride, s, product)

    per_core(where_ref, codes_ref, range(4), 4, for_up, for_down)
    for n, out in enumerate((o0, o1, o2, o3)):
        out[...] = acc[n].astype(jnp.bfloat16)


def grads_kernel(slots, where_ref, codes_ref, acts, came, slope, *refs):
    picked = refs[-1]
    for d, grads in zip(slots, refs):

        def for_up(d, r, n):
            pick(acts, picked.at[n], *spots(where_ref, codes_ref, d, r))
            mine = pulled(came, slope, column(where_ref, d, r))
            grad = lax.dot_general(
                picked[n], mine, (((0,), (0,)), ((), ())), preferred_element_type=jnp.float32
            )
            grads[r] = grad.astype(jnp.bfloat16).reshape(8, BLK, BLK)

        def for_down(d, r, n):
            pick(acts, picked.at[n], *spots(where_ref, codes_ref, d, r))
            grad = lax.dot_general(
                came[column(where_ref, d, r)],
                picked[n],
                (((0,), (0,)), ((), ())),
                preferred_element_type=jnp.float32,
            ).astype(jnp.bfloat16)
            for s in range(8):
                grads[r, s] = grad[:, s * BLK : (s + 1) * BLK]

        per_core(where_ref, codes_ref, (d,), 2, for_up, for_down)


SMEM = pl.BlockSpec(memory_space=pltpu.SMEM)
VMEM = pl.BlockSpec(memory_space=pltpu.VMEM)
ANY = pl.BlockSpec(memory_space=pl.ANY)
ACTS = (RING, RING, 2, BLK, 512)
WEIGHTS = (RING, 2, 8, BLK, BLK)


CHUNK = jax.ShapeDtypeStruct(ACTS[1:], jnp.bfloat16)
GRAD = jax.ShapeDtypeStruct(WEIGHTS[1:], jnp.bfloat16)
HIDDEN = (8, 512, BLK)


def cost(flops, moved):
    return pl.CostEstimate(flops=flops, bytes_accessed=moved, transcendentals=0)


def enter(where, codes, acts, weights):
    return pl.pallas_call(
        enter_kernel,
        out_shape=[
            jax.ShapeDtypeStruct(ACTS, jnp.bfloat16),
            jax.ShapeDtypeStruct(WEIGHTS, jnp.bfloat16),
            jax.ShapeDtypeStruct(HIDDEN, jnp.bfloat16),
            jax.ShapeDtypeStruct(HIDDEN, jnp.float32),
        ],
        in_specs=[SMEM, SMEM] + [ANY] * 8,
        out_specs=[VMEM] * 4,
        scratch_shapes=[
            pltpu.VMEM((4, 512, 8 * BLK), jnp.bfloat16),
            pltpu.SemaphoreType.DMA((8,)),
        ],
        compiler_params=pltpu.CompilerParams(vmem_limit_bytes=10 << 20),
        cost_estimate=cost(1 << 30, 8 << 20),
        name="enter",
    )(where, codes, *acts, *weights)


def sums(where, codes, weights, came, slope):
    return pl.pallas_call(
        sums_kernel,
        out_shape=[CHUNK] * 4,
        in_specs=[SMEM, SMEM] + [VMEM] * 3,
        out_specs=[VMEM] * 4,
        scratch_shapes=[pltpu.VMEM(ACTS, jnp.float32)],
        compiler_params=pltpu.CompilerParams(vmem_limit_bytes=14 << 20),
        cost_estimate=cost(1 << 30, 8 << 20),
        name="sums",
    )(where, codes, weights, came, slope)


def block_grads(slots, where, codes, acts, came, slope):
    return pl.pallas_call(
        functools.partial(grads_kernel, slots),
        out_shape=[GRAD] * len(slots),
        in_specs=[SMEM, SMEM] + [VMEM] * 3,
        out_specs=[VMEM] * len(slots),
        scratch_shapes=[pltpu.VMEM((2, 512, 8 * BLK), jnp.bfloat16)],
        compiler_params=pltpu.CompilerParams(vmem_limit_bytes=10 << 20),
        cost_estimate=cost(1 << 29, 8 << 20),
        name="grads",
    )(where, codes, acts, came, slope)


def per_device(tokens, up_weight, up_rows, down_weight, down_cols, grad_out):
    x, y, z = (lax.axis_index(name) for name in ("x", "y", "z"))
    core = lax.axis_index("core")
    up = core == 0

    def first(stage):
        return lambda values, step: mixed_shift(values, step, stage)

    kept = jnp.where(up, tokens, grad_out)
    acts = jnp.stack([kept, swap(jnp.where(up, grad_out, tokens))])
    kept = jnp.where(up, up_weight[0], down_weight[0])
    weights = jnp.stack([kept, swap(jnp.where(up, down_weight[0], up_weight[0]))])

    up_ids = lax.dynamic_index_in_dim(up_rows.reshape(4, 4, 8), x, axis=1, keepdims=False)
    down_ids = lax.dynamic_index_in_dim(down_cols.reshape(4, 4, 8), x, axis=1, keepdims=False)
    ids = jnp.stack([jnp.where(up, up_ids, down_ids), swap(jnp.where(up, down_ids, up_ids))])
    codes = ((y - (ids >> 3)) & 3) * 8 + (((ids >> 2) & 1) ^ core) * 4 + (ids & 3)
    where = jnp.stack([core, z])

    acts = gather(jnp.stack(gather(acts, first(True))), first(False))
    weights = gather(weights, z_shift)

    acts, weights, sent, slope = enter(where, codes, acts, weights)
    came = swap(sent)
    chunks = sums(where, codes, weights, came, slope)
    grads_1, grads_3 = block_grads((1, 3), where, codes, acts, came, slope)
    grads_2, grads_0 = block_grads((2, 0), where, codes, acts, came, slope)
    grads = [grads_0, grads_1, grads_2, grads_3]

    summed = reduce(chunks, first(False)).astype(jnp.bfloat16)
    final = reduce([summed[n] for n in range(RING)], first(True)).astype(jnp.bfloat16)
    grad_scale = 1.0 / math.sqrt(tokens.shape[0] * lax.axis_size("z") * lax.axis_size("x"))
    scaled = (reduce(grads, z_shift) * grad_scale).astype(jnp.bfloat16)
    came_act = swap(final[1])
    came_grad = swap(scaled[1])
    layer_out = jnp.where(up, came_act, final[0])
    grad_tokens = jnp.where(up, final[0], came_act)
    grad_up = jnp.where(up, scaled[0], came_grad)
    grad_down = jnp.where(up, came_grad, scaled[0])
    return (layer_out, grad_tokens, grad_up[None], grad_down[None])


def solution(mesh):
    grid = Mesh(mesh.devices.reshape(4, 4, 4, 2), ("z", "x", "y", "core"))
    row, col = ("z", "x"), ("y", "core")
    acts, ids = P(row, col), P(col, None)
    blocks = P(col + row, None, None, None)
    return jax.shard_map(
        per_device,
        mesh=grid,
        in_specs=(acts, blocks, ids, blocks, ids, acts),
        out_specs=(acts, acts, blocks, blocks),
        check_vma=False,
    )
```

```python
import functools
import math

import jax
import jax.numpy as jnp
from jax import lax
from jax.experimental import pallas as pl
from jax.experimental.pallas import tpu as pltpu
from jax.sharding import Mesh
from jax.sharding import PartitionSpec as P

RING = 4
BLK = 128
STEPS = (1, 3, 2)
GELU_SCALE = math.sqrt(2.0 / math.pi)
GELU_CUBIC = 0.044715
MIXED = ("x", "y", "core")


def place(x, y, core):
    return (x % RING * RING + y % RING) * 2 + core


def mixed_pairs(step, first):
    pairs = []
    for x in range(RING):
        for y in range(RING):
            for core in range(2):
                dx, dy = (step, 0) if (core == 0) == first else (0, step)
                pairs.append((place(x, y, core), place(x + dx, y + dy, core)))
    return pairs


def mixed_shift(values, step, first):
    return lax.ppermute(values, MIXED, mixed_pairs(step, first))


def z_shift(values, step):
    pairs = [(i * 2, (i + step) % RING * 2) for i in range(RING)]
    pairs += [(i * 2 + 1, (i - step) % RING * 2 + 1) for i in range(RING)]
    return lax.ppermute(values, ("z", "core"), pairs)


def swap(values):
    return lax.ppermute(values, "core", [(0, 1), (1, 0)])


def gather(values, shift):
    slots = {0: values}
    for step in STEPS:
        slots[step] = shift(values, step)
    return [slots[step] for step in range(RING)]


def reduce(chunks, shift, steps=STEPS):
    parts = [chunks[0]]
    for step in steps:
        parts.append(shift(chunks[step], RING - step))
    return sum(part.astype(jnp.float32) for part in parts)


def load(acts_refs, weight_refs, acts, weights, sems):
    copies = [(src, acts.at[n]) for n, src in enumerate(acts_refs)]
    copies += [(src, weights.at[n]) for n, src in enumerate(weight_refs)]
    copies = [
        pltpu.make_async_copy(src, dst, sems.at[n]) for n, (src, dst) in enumerate(copies)
    ]
    for copy in copies:
        copy.start()
    return copies


def from_z(where_ref, d):
    return (where_ref[1] + jnp.where(where_ref[0] == 0, -d, d)) & 3


def column(where_ref, d, r):
    return from_z(where_ref, d) * 2 + (r ^ where_ref[0])


def spots(where_ref, codes_ref, d, r):
    core = where_ref[0]
    z = from_z(where_ref, d)
    out = []
    for s in range(8):
        code = codes_ref[r, z, s]
        slot = code >> 3
        first = jnp.where(core == 0, slot * 4, slot)
        cols = pl.ds(pl.multiple_of((code & 3) * BLK, BLK), BLK)
        out.append((first, (code >> 2) & 1, cols))
    return out, jnp.where(core == 0, 1, 4)


def pick(acts, picked, places, stride):
    for s, (first, half, cols) in enumerate(places):
        for q in range(RING):
            picked[q * BLK : (q + 1) * BLK, s * BLK : (s + 1) * BLK] = acts[
                (first + q * stride) >> 2, (first + q * stride) & 3, half, :, cols
            ]


def per_core(where_ref, codes_ref, columns, unroll, for_up, for_down):
    def run(step_function):
        def body(turn, carry):
            for n in range(unroll):
                step = turn * unroll + n
                step_function(columns[0] + (step >> 1), step & 1, n)
            return carry

        lax.fori_loop(0, 2 * len(columns) // unroll, body, 0)

    @pl.when(where_ref[0] == 0)
    def _():
        run(for_up)

    @pl.when(where_ref[0] == 1)
    def _():
        run(for_down)


def enter_kernel(
    where_ref, codes_ref, a0, a1, a2, a3, w0, w1, w2, w3,
    acts, weights, sent, slope, acc, picked, sems,
):
    copies = load((a0, a1, a2, a3), (w0, w1, w2, w3), acts, weights, sems)
    acc[...] = jnp.zeros_like(acc)
    for copy in copies:
        copy.wait()

    def for_up(d, r, n):
        at = column(where_ref, d, r)
        pick(acts, picked.at[n], *spots(where_ref, codes_ref, d, r))
        pre = jnp.dot(
            picked[n], weights[d, r].reshape(8 * BLK, BLK), preferred_element_type=jnp.float32
        )
        square = pre * pre
        t = jnp.tanh(pre * (GELU_SCALE + GELU_SCALE * GELU_CUBIC * square))
        half = 0.5 + 0.5 * t
        sent[at] = (pre * half).astype(jnp.bfloat16)
        slope[at] = half + pre * (half - half * t) * (
            GELU_SCALE + 3.0 * GELU_SCALE * GELU_CUBIC * square
        )

    def for_down(d, r, n):
        at = column(where_ref, d, r)
        pick(acts, picked.at[n], *spots(where_ref, codes_ref, d, r))
        flat = jnp.concatenate([weights[d, r, s] for s in range(8)], axis=1)
        sent[at] = lax.dot_general(
            picked[n], flat, (((1,), (1,)), ((), ())), preferred_element_type=jnp.float32
        ).astype(jnp.bfloat16)

    per_core(where_ref, codes_ref, range(4), 4, for_up, for_down)


def pulled(came, slope, row):
    return (came[row].astype(jnp.float32) * slope[row]).astype(jnp.bfloat16)


def sums_kernel(where_ref, codes_ref, weights, came, slope, zeros, acc, o0, o1, o2, o3):
    def scatter(places, stride, s, product):
        for n in range(2):
            first, half, cols = places[s + n]
            for q in range(RING):
                at = first + q * stride
                acc[at >> 2, at & 3, half, :, cols] += product[
                    q * BLK : (q + 1) * BLK, n * BLK : (n + 1) * BLK
                ]

    def for_up(d, r, n):
        mine = pulled(came, slope, column(where_ref, d, r))
        places, stride = spots(where_ref, codes_ref, d, r)
        for s in range(0, 8, 2):
            pair = weights[d, r, s : s + 2].reshape(2 * BLK, BLK)
            product = lax.dot_general(
                mine, pair, (((1,), (1,)), ((), ())), preferred_element_type=jnp.float32
            )
            scatter(places, stride, s, product)

    def for_down(d, r, n):
        mine = came[column(where_ref, d, r)]
        places, stride = spots(where_ref, codes_ref, d, r)
        for s in range(0, 8, 2):
            pair = jnp.concatenate([weights[d, r, s], weights[d, r, s + 1]], axis=1)
            product = jnp.dot(mine, pair, preferred_element_type=jnp.float32)
            scatter(places, stride, s, product)

    per_core(where_ref, codes_ref, range(4), 4, for_up, for_down)
    for n, out in enumerate((o0, o1, o2, o3)):
        out[...] = acc[n].astype(jnp.bfloat16)


def grads_kernel(slots, where_ref, codes_ref, acts, came, slope, *refs):
    picked = refs[-1]
    for d, grads in zip(slots, refs):

        def for_up(d, r, n):
            pick(acts, picked.at[n], *spots(where_ref, codes_ref, d, r))
            mine = pulled(came, slope, column(where_ref, d, r))
            grad = lax.dot_general(
                picked[n], mine, (((0,), (0,)), ((), ())), preferred_element_type=jnp.float32
            )
            grads[r] = grad.astype(jnp.bfloat16).reshape(8, BLK, BLK)

        def for_down(d, r, n):
            pick(acts, picked.at[n], *spots(where_ref, codes_ref, d, r))
            grad = lax.dot_general(
                came[column(where_ref, d, r)],
                picked[n],
                (((0,), (0,)), ((), ())),
                preferred_element_type=jnp.float32,
            ).astype(jnp.bfloat16)
            for s in range(8):
                grads[r, s] = grad[:, s * BLK : (s + 1) * BLK]

        per_core(where_ref, codes_ref, (d,), 2, for_up, for_down)


SMEM = pl.BlockSpec(memory_space=pltpu.SMEM)
VMEM = pl.BlockSpec(memory_space=pltpu.VMEM)
ANY = pl.BlockSpec(memory_space=pl.ANY)
ACTS = (RING, RING, 2, BLK, 512)
WEIGHTS = (RING, 2, 8, BLK, BLK)


CHUNK = jax.ShapeDtypeStruct(ACTS[1:], jnp.bfloat16)
GRAD = jax.ShapeDtypeStruct(WEIGHTS[1:], jnp.bfloat16)
HIDDEN = (8, 512, BLK)


def cost(flops, moved):
    return pl.CostEstimate(flops=flops, bytes_accessed=moved, transcendentals=0)


def enter(where, codes, acts, weights):
    return pl.pallas_call(
        enter_kernel,
        out_shape=[
            jax.ShapeDtypeStruct(ACTS, jnp.bfloat16),
            jax.ShapeDtypeStruct(WEIGHTS, jnp.bfloat16),
            jax.ShapeDtypeStruct(HIDDEN, jnp.bfloat16),
            jax.ShapeDtypeStruct(HIDDEN, jnp.float32),
            jax.ShapeDtypeStruct(ACTS, jnp.float32),
        ],
        in_specs=[SMEM, SMEM] + [ANY] * 8,
        out_specs=[VMEM] * 5,
        scratch_shapes=[
            pltpu.VMEM((4, 512, 8 * BLK), jnp.bfloat16),
            pltpu.SemaphoreType.DMA((8,)),
        ],
        compiler_params=pltpu.CompilerParams(vmem_limit_bytes=10 << 20),
        cost_estimate=cost(1 << 30, 8 << 20),
        name="enter",
    )(where, codes, *acts, *weights)


def sums(where, codes, weights, came, slope, zeros):
    return pl.pallas_call(
        sums_kernel,
        out_shape=[jax.ShapeDtypeStruct(ACTS, jnp.float32)] + [CHUNK] * 4,
        in_specs=[SMEM, SMEM] + [VMEM] * 4,
        out_specs=[VMEM] * 5,
        input_output_aliases={5: 0},
        compiler_params=pltpu.CompilerParams(vmem_limit_bytes=14 << 20),
        cost_estimate=cost(1 << 30, 8 << 20),
        name="sums",
    )(where, codes, weights, came, slope, zeros)[1:]


def block_grads(slots, where, codes, acts, came, slope):
    return pl.pallas_call(
        functools.partial(grads_kernel, slots),
        out_shape=[GRAD] * len(slots),
        in_specs=[SMEM, SMEM] + [VMEM] * 3,
        out_specs=[VMEM] * len(slots),
        scratch_shapes=[pltpu.VMEM((2, 512, 8 * BLK), jnp.bfloat16)],
        compiler_params=pltpu.CompilerParams(vmem_limit_bytes=10 << 20),
        cost_estimate=cost(1 << 29, 8 << 20),
        name="grads",
    )(where, codes, acts, came, slope)


def per_device(tokens, up_weight, up_rows, down_weight, down_cols, grad_out):
    x, y, z = (lax.axis_index(name) for name in ("x", "y", "z"))
    core = lax.axis_index("core")
    up = core == 0

    def first(stage):
        return lambda values, step: mixed_shift(values, step, stage)

    kept = jnp.where(up, tokens, grad_out)
    acts = jnp.stack([kept, swap(jnp.where(up, grad_out, tokens))])
    kept = jnp.where(up, up_weight[0], down_weight[0])
    weights = jnp.stack([kept, swap(jnp.where(up, down_weight[0], up_weight[0]))])

    up_ids = lax.dynamic_index_in_dim(up_rows.reshape(4, 4, 8), x, axis=1, keepdims=False)
    down_ids = lax.dynamic_index_in_dim(down_cols.reshape(4, 4, 8), x, axis=1, keepdims=False)
    ids = jnp.stack([jnp.where(up, up_ids, down_ids), swap(jnp.where(up, down_ids, up_ids))])
    codes = ((y - (ids >> 3)) & 3) * 8 + (((ids >> 2) & 1) ^ core) * 4 + (ids & 3)
    where = jnp.stack([core, z])

    acts = gather(jnp.stack(gather(acts, first(True))), first(False))
    weights = gather(weights, z_shift)

    acts, weights, sent, slope, zeros = enter(where, codes, acts, weights)
    came = swap(sent)
    chunks = sums(where, codes, weights, came, slope, zeros)
    grads_2, grads_1 = block_grads((2, 1), where, codes, acts, came, slope)
    grads_3, grads_0 = block_grads((3, 0), where, codes, acts, came, slope)
    grads = [grads_0, grads_1, grads_2, grads_3]

    summed = reduce(chunks, first(False)).astype(jnp.bfloat16)
    final = reduce([summed[n] for n in range(RING)], first(True)).astype(jnp.bfloat16)
    grad_scale = 1.0 / math.sqrt(tokens.shape[0] * lax.axis_size("z") * lax.axis_size("x"))
    scaled = (reduce(grads, z_shift, (2, 1, 3)) * grad_scale).astype(jnp.bfloat16)
    came_grad = swap(scaled[1])
    grad_up = jnp.where(up, scaled[0], came_grad)
    grad_down = jnp.where(up, came_grad, scaled[0])
    came_act = swap(final[1])
    layer_out = jnp.where(up, came_act, final[0])
    grad_tokens = jnp.where(up, final[0], came_act)
    return (layer_out, grad_tokens, grad_up[None], grad_down[None])


def solution(mesh):
    grid = Mesh(mesh.devices.reshape(4, 4, 4, 2), ("z", "x", "y", "core"))
    row, col = ("z", "x"), ("y", "core")
    acts, ids = P(row, col), P(col, None)
    blocks = P(col + row, None, None, None)
    return jax.shard_map(
        per_device,
        mesh=grid,
        in_specs=(acts, blocks, ids, blocks, ids, acts),
        out_specs=(acts, acts, blocks, blocks),
        check_vma=False,
    )
```

```python
import functools
import math

import jax
import jax.numpy as jnp
from jax import lax
from jax.experimental import pallas as pl
from jax.experimental.pallas import tpu as pltpu
from jax.sharding import Mesh
from jax.sharding import PartitionSpec as P

RING = 4
BLK = 128
STEPS = (1, 3, 2)
GELU_SCALE = math.sqrt(2.0 / math.pi)
GELU_CUBIC = 0.044715
MIXED = ("x", "y", "core")


def place(x, y, core):
    return (x % RING * RING + y % RING) * 2 + core


def mixed_pairs(step, first):
    pairs = []
    for x in range(RING):
        for y in range(RING):
            for core in range(2):
                dx, dy = (step, 0) if (core == 0) == first else (0, step)
                pairs.append((place(x, y, core), place(x + dx, y + dy, core)))
    return pairs


def mixed_shift(values, step, first):
    return lax.ppermute(values, MIXED, mixed_pairs(step, first))


def z_shift(values, step):
    pairs = [(i * 2, (i + step) % RING * 2) for i in range(RING)]
    pairs += [(i * 2 + 1, (i - step) % RING * 2 + 1) for i in range(RING)]
    return lax.ppermute(values, ("z", "core"), pairs)


def swap(values):
    return lax.ppermute(values, "core", [(0, 1), (1, 0)])


def gather(values, shift):
    slots = {0: values}
    for step in STEPS:
        slots[step] = shift(values, step)
    return [slots[step] for step in range(RING)]


def reduce(chunks, shift, steps=STEPS):
    parts = [chunks[0]]
    for step in steps:
        parts.append(shift(chunks[step], RING - step))
    return sum(part.astype(jnp.float32) for part in parts)


def load(acts_refs, weight_refs, acts, weights, sems):
    copies = [(src, acts.at[n]) for n, src in enumerate(acts_refs)]
    copies += [(src, weights.at[n]) for n, src in enumerate(weight_refs)]
    copies = [
        pltpu.make_async_copy(src, dst, sems.at[n]) for n, (src, dst) in enumerate(copies)
    ]
    for copy in copies:
        copy.start()
    return copies


def from_z(where_ref, d):
    return (where_ref[1] + jnp.where(where_ref[0] == 0, -d, d)) & 3


def column(where_ref, d, r):
    return from_z(where_ref, d) * 2 + (r ^ where_ref[0])


def spots(where_ref, codes_ref, d, r):
    core = where_ref[0]
    z = from_z(where_ref, d)
    out = []
    for s in range(8):
        code = codes_ref[r, z, s]
        slot = code >> 3
        first = jnp.where(core == 0, slot * 4, slot)
        cols = pl.ds(pl.multiple_of((code & 3) * BLK, BLK), BLK)
        out.append((first, (code >> 2) & 1, cols))
    return out, jnp.where(core == 0, 1, 4)


def pick(acts, picked, places, stride):
    for s, (first, half, cols) in enumerate(places):
        for q in range(RING):
            picked[q * BLK : (q + 1) * BLK, s * BLK : (s + 1) * BLK] = acts[
                (first + q * stride) >> 2, (first + q * stride) & 3, half, :, cols
            ]


def per_core(where_ref, codes_ref, columns, unroll, for_up, for_down):
    def run(step_function):
        def body(turn, carry):
            for n in range(unroll):
                step = turn * unroll + n
                step_function(columns[0] + (step >> 1), step & 1, n)
            return carry

        lax.fori_loop(0, 2 * len(columns) // unroll, body, 0)

    @pl.when(where_ref[0] == 0)
    def _():
        run(for_up)

    @pl.when(where_ref[0] == 1)
    def _():
        run(for_down)


def enter_kernel(
    where_ref, codes_ref, a0, a1, a2, a3, w0, w1, w2, w3,
    acts, weights, sent, slope, acc, picked, sems,
):
    copies = load((a0, a1, a2, a3), (w0, w1, w2, w3), acts, weights, sems)
    acc[...] = jnp.zeros_like(acc)
    for copy in copies:
        copy.wait()

    def for_up(d, r, n):
        at = column(where_ref, d, r)
        pick(acts, picked.at[n], *spots(where_ref, codes_ref, d, r))
        pre = jnp.dot(
            picked[n], weights[d, r].reshape(8 * BLK, BLK), preferred_element_type=jnp.float32
        )
        square = pre * pre
        t = jnp.tanh(pre * (GELU_SCALE + GELU_SCALE * GELU_CUBIC * square))
        half = 0.5 + 0.5 * t
        sent[at] = (pre * half).astype(jnp.bfloat16)
        slope[at] = half + pre * (half - half * t) * (
            GELU_SCALE + 3.0 * GELU_SCALE * GELU_CUBIC * square
        )

    def for_down(d, r, n):
        at = column(where_ref, d, r)
        pick(acts, picked.at[n], *spots(where_ref, codes_ref, d, r))
        flat = jnp.concatenate([weights[d, r, s] for s in range(8)], axis=1)
        sent[at] = lax.dot_general(
            picked[n], flat, (((1,), (1,)), ((), ())), preferred_element_type=jnp.float32
        ).astype(jnp.bfloat16)

    per_core(where_ref, codes_ref, range(4), 4, for_up, for_down)


def pulled(came, slope, row):
    return (came[row].astype(jnp.float32) * slope[row]).astype(jnp.bfloat16)


def sums_kernel(where_ref, codes_ref, weights, came, slope, zeros, acc, o0, o1, o2, o3):
    def scatter(places, stride, s, product):
        for n in range(2):
            first, half, cols = places[s + n]
            for q in range(RING):
                at = first + q * stride
                acc[at >> 2, at & 3, half, :, cols] += product[
                    q * BLK : (q + 1) * BLK, n * BLK : (n + 1) * BLK
                ]

    def for_up(d, r, n):
        mine = pulled(came, slope, column(where_ref, d, r))
        places, stride = spots(where_ref, codes_ref, d, r)
        for s in range(0, 8, 2):
            pair = weights[d, r, s : s + 2].reshape(2 * BLK, BLK)
            product = lax.dot_general(
                mine, pair, (((1,), (1,)), ((), ())), preferred_element_type=jnp.float32
            )
            scatter(places, stride, s, product)

    def for_down(d, r, n):
        mine = came[column(where_ref, d, r)]
        places, stride = spots(where_ref, codes_ref, d, r)
        for s in range(0, 8, 2):
            pair = jnp.concatenate([weights[d, r, s], weights[d, r, s + 1]], axis=1)
            product = jnp.dot(mine, pair, preferred_element_type=jnp.float32)
            scatter(places, stride, s, product)

    per_core(where_ref, codes_ref, range(4), 4, for_up, for_down)
    for n, out in enumerate((o0, o1, o2, o3)):
        out[...] = acc[n].astype(jnp.bfloat16)


def grads_kernel(slots, where_ref, codes_ref, acts, came, slope, *refs):
    picked = refs[-1]
    for d, grads in zip(slots, refs):

        def for_up(d, r, n):
            pick(acts, picked.at[n], *spots(where_ref, codes_ref, d, r))
            mine = pulled(came, slope, column(where_ref, d, r))
            grad = lax.dot_general(
                picked[n], mine, (((0,), (0,)), ((), ())), preferred_element_type=jnp.float32
            )
            grads[r] = grad.astype(jnp.bfloat16).reshape(8, BLK, BLK)

        def for_down(d, r, n):
            pick(acts, picked.at[n], *spots(where_ref, codes_ref, d, r))
            grad = lax.dot_general(
                came[column(where_ref, d, r)],
                picked[n],
                (((0,), (0,)), ((), ())),
                preferred_element_type=jnp.float32,
            ).astype(jnp.bfloat16)
            for s in range(8):
                grads[r, s] = grad[:, s * BLK : (s + 1) * BLK]

        per_core(where_ref, codes_ref, (d,), 2, for_up, for_down)


SMEM = pl.BlockSpec(memory_space=pltpu.SMEM)
VMEM = pl.BlockSpec(memory_space=pltpu.VMEM)
ANY = pl.BlockSpec(memory_space=pl.ANY)
ACTS = (RING, RING, 2, BLK, 512)
WEIGHTS = (RING, 2, 8, BLK, BLK)


CHUNK = jax.ShapeDtypeStruct(ACTS[1:], jnp.bfloat16)
GRAD = jax.ShapeDtypeStruct(WEIGHTS[1:], jnp.bfloat16)
HIDDEN = (8, 512, BLK)


def cost(flops, moved):
    return pl.CostEstimate(flops=flops, bytes_accessed=moved, transcendentals=0)


def enter(where, codes, acts, weights):
    return pl.pallas_call(
        enter_kernel,
        out_shape=[
            jax.ShapeDtypeStruct(ACTS, jnp.bfloat16),
            jax.ShapeDtypeStruct(WEIGHTS, jnp.bfloat16),
            jax.ShapeDtypeStruct(HIDDEN, jnp.bfloat16),
            jax.ShapeDtypeStruct(HIDDEN, jnp.float32),
            jax.ShapeDtypeStruct(ACTS, jnp.float32),
        ],
        in_specs=[SMEM, SMEM] + [ANY] * 8,
        out_specs=[VMEM] * 5,
        scratch_shapes=[
            pltpu.VMEM((4, 512, 8 * BLK), jnp.bfloat16),
            pltpu.SemaphoreType.DMA((8,)),
        ],
        compiler_params=pltpu.CompilerParams(vmem_limit_bytes=10 << 20),
        cost_estimate=cost(1 << 30, 8 << 20),
        name="enter",
    )(where, codes, *acts, *weights)


def sums(where, codes, weights, came, slope, zeros):
    return pl.pallas_call(
        sums_kernel,
        out_shape=[jax.ShapeDtypeStruct(ACTS, jnp.float32)] + [CHUNK] * 4,
        in_specs=[SMEM, SMEM] + [VMEM] * 4,
        out_specs=[VMEM] * 5,
        input_output_aliases={5: 0},
        compiler_params=pltpu.CompilerParams(vmem_limit_bytes=14 << 20),
        cost_estimate=cost(1 << 30, 8 << 20),
        name="sums",
    )(where, codes, weights, came, slope, zeros)[1:]


def block_grads(slots, where, codes, acts, came, slope):
    return pl.pallas_call(
        functools.partial(grads_kernel, slots),
        out_shape=[GRAD] * len(slots),
        in_specs=[SMEM, SMEM] + [VMEM] * 3,
        out_specs=[VMEM] * len(slots),
        scratch_shapes=[pltpu.VMEM((2, 512, 8 * BLK), jnp.bfloat16)],
        compiler_params=pltpu.CompilerParams(vmem_limit_bytes=10 << 20),
        cost_estimate=cost(1 << 29, 8 << 20),
        name="grads",
    )(where, codes, acts, came, slope)


def per_device(tokens, up_weight, up_rows, down_weight, down_cols, grad_out):
    x, y, z = (lax.axis_index(name) for name in ("x", "y", "z"))
    core = lax.axis_index("core")
    up = core == 0

    def first(stage):
        return lambda values, step: mixed_shift(values, step, stage)

    kept = jnp.where(up, tokens, grad_out)
    acts = jnp.stack([kept, swap(jnp.where(up, grad_out, tokens))])
    kept = jnp.where(up, up_weight[0], down_weight[0])
    weights = jnp.stack([kept, swap(jnp.where(up, down_weight[0], up_weight[0]))])

    up_ids = lax.dynamic_index_in_dim(up_rows.reshape(4, 4, 8), x, axis=1, keepdims=False)
    down_ids = lax.dynamic_index_in_dim(down_cols.reshape(4, 4, 8), x, axis=1, keepdims=False)
    ids = jnp.stack([jnp.where(up, up_ids, down_ids), swap(jnp.where(up, down_ids, up_ids))])
    codes = ((y - (ids >> 3)) & 3) * 8 + (((ids >> 2) & 1) ^ core) * 4 + (ids & 3)
    where = jnp.stack([core, z])

    acts = gather(jnp.stack(gather(acts, first(True))), first(False))
    weights = gather(weights, z_shift)

    acts, weights, sent, slope, zeros = enter(where, codes, acts, weights)
    came = swap(sent)
    chunks = sums(where, codes, weights, came, slope, zeros)
    grads_2, grads_1 = block_grads((2, 1), where, codes, acts, came, slope)
    grads_3, grads_0 = block_grads((3, 0), where, codes, acts, came, slope)
    grads = [grads_0, grads_1, grads_2, grads_3]

    summed = reduce(chunks, first(False)).astype(jnp.bfloat16)
    final = reduce([summed[n] for n in range(RING)], first(True), (2, 1, 3)).astype(jnp.bfloat16)
    grad_scale = 1.0 / math.sqrt(tokens.shape[0] * lax.axis_size("z") * lax.axis_size("x"))
    scaled = (reduce(grads, z_shift, (2, 1, 3)) * grad_scale).astype(jnp.bfloat16)
    came_grad = swap(scaled[1])
    grad_up = jnp.where(up, scaled[0], came_grad)
    grad_down = jnp.where(up, came_grad, scaled[0])
    came_act = swap(final[1])
    layer_out = jnp.where(up, came_act, final[0])
    grad_tokens = jnp.where(up, final[0], came_act)
    return (layer_out, grad_tokens, grad_up[None], grad_down[None])


def solution(mesh):
    grid = Mesh(mesh.devices.reshape(4, 4, 4, 2), ("z", "x", "y", "core"))
    row, col = ("z", "x"), ("y", "core")
    acts, ids = P(row, col), P(col, None)
    blocks = P(col + row, None, None, None)
    return jax.shard_map(
        per_device,
        mesh=grid,
        in_specs=(acts, blocks, ids, blocks, ids, acts),
        out_specs=(acts, acts, blocks, blocks),
        check_vma=False,
    )
```
